128 devices in a mesh: section: 16 (over z_hi, y, core), seq: 8 (over x, z_lo).
Axes of the slice: x: 4, y: 4, z: 4 (z_hi: 2, z_lo: 2; z = z_hi * 2 + z_lo), core: 2. Of those that a mesh axis runs over, the one named last changes fastest.
Arguments:
- forward_rows: bfloat16 [16, 1024, 4096], P('section', 'seq'), may hold values from -54 to 54
- saved_rows: bfloat16 [16, 1024, 4096], P('section', 'seq'), may hold values from -54 to 54
- output_grad: bfloat16 [16, 1024, 4096], P('section', 'seq'), may hold values from -6 to 6
- forward_docs: int32 [16, 1024], replicated, may hold values from 0 to 3, never falling along the last dimension, each value on 1 to 512 neighbouring positions
- backward_docs: int32 [16, 1024], replicated, may hold values from 0 to 3, never falling along the last dimension, each value on 1 to 512 neighbouring positions
- norm_gain: float32 [16, 4096], P('section'), may hold values from 0.7 to 8
- query_weight: bfloat16 [16, 4096, 4096], P('section', None, 'seq'), may hold values from -0.09375 to 0.09375
- key_matrix: bfloat16 [16, 4096, 1024], P('section', None, 'seq'), may hold values from -0.09375 to 0.09375
- value_matrix: bfloat16 [16, 4096, 1024], P('section', None, 'seq'), may hold values from -0.09375 to 0.09375
Outputs:
- section_output: bfloat16 [16, 1024, 4096], P('section', 'seq')
- input_grad: bfloat16 [16, 1024, 4096], P('section', 'seq')
The draws below stay inside these ranges and needn't reach their ends.
Inputs may be any that keep to these rules, and one draw needn't show every extreme that they name: `forward_docs`: document ids never fall along a row; every document holds at most 512 tokens and some document of each row holds exactly that many. `backward_docs`: document ids never fall along a row; every document holds at most 512 tokens and some document of each row holds exactly that many.
All inputs are finite; a program needn't handle non-finite values.
Results may differ from the reference program's by a relative error of at most 0.017.
The reference program's roundings to bfloat16 on the way count: a program that leaves them out, or rounds other values in their place, can miss the bound.
Values may be sent and summed in bfloat16 or wider, within the bound.
A program may use at most 192 MiB of HBM per device.

```python
import math
import jax
import jax.numpy as jnp
import numpy as np
from jax import lax

MODEL_WIDTH = 4096
HQ = 32
KEY_VALUE_HEADS = 8
HEAD_SIZE = 128
QUERIES_PER_KEY = 4
SEQLEN = 1024
N_SECTION = 16
N_SEQ = 8


def scaled_rows(key):
    base_key, col_key, row_key = jax.random.split(key, 3)
    base = jnp.clip(jax.random.normal(base_key, (N_SECTION, SEQLEN, MODEL_WIDTH)), -6.0, 6.0)
    col_scale = jnp.exp(jax.random.uniform(col_key, (N_SECTION, 1, MODEL_WIDTH), minval=math.log(0.3), maxval=math.log(3.0)))
    row_scale = jnp.exp(jax.random.uniform(row_key, (N_SECTION, SEQLEN, 1), minval=math.log(0.3), maxval=math.log(3.0)))
    return (base * col_scale * row_scale).astype(jnp.float32)


def draw_forward_rows(key, part):
    return scaled_rows(jax.random.fold_in(key, 11)).astype(jnp.bfloat16)


def draw_saved_rows(key, part):
    return scaled_rows(jax.random.fold_in(key, 12)).astype(jnp.bfloat16)


def draw_norm_gain(key, part):
    gain_key = jax.random.fold_in(key, 31)
    return (1.0 + 0.3 * jax.random.uniform(gain_key, (N_SECTION, MODEL_WIDTH), minval=-1.0, maxval=1.0)).astype(jnp.float32)


def level_of(rng, shape, cuts, least, largest):
    level = 1.0
    for position, parts in cuts:
        draws = jax.random.uniform(jax.random.fold_in(jax.random.fold_in(rng, 6), position), (parts,), jnp.float32, least / len(cuts), largest / len(cuts))
        level = level * jnp.repeat(jnp.exp(draws), shape[position] // parts).reshape((-1,) + (1,) * (len(shape) - 1 - position))
    return level


def split_up(amount, total, reach, skew):
    portions = [(1 << 20) // math.isqrt(standing ** skew) + 1 for standing in range(2, amount + 1)]
    rest, holding = total - reach - (amount - 1), [1] * (amount - 1)
    while rest > 0:
        free = [i for i in range(amount - 1) if holding[i] < reach]
        whole, left = sum([portions[i] for i in free]), rest
        for i in free:
            more = min(reach - holding[i], max(1, left * portions[i] // whole), rest)
            holding[i] = holding[i] + more
            rest = rest - more
    return np.array([reach] + holding)


def ragged_sizes(stream_key, amount, total, reach, skew):
    if amount == 2:
        one = jax.random.randint(stream_key, (), max(1, total - reach), min(reach, total - 1) + 1)
        return jnp.stack([one, total - one])
    sizes = jnp.asarray(split_up(amount, total, reach, skew), jnp.int32)
    twos = (amount - 1) // 2
    donor, receiver = sizes[1:1 + 2 * twos:2], sizes[2:2 + 2 * twos:2]
    margin = jnp.minimum(donor - 1, reach - receiver)
    shifted = jax.random.randint(jax.random.fold_in(stream_key, 1), (twos,), 0, 1 << 20) % (margin + 1)
    sizes = sizes.at[1:1 + 2 * twos:2].set(donor - shifted).at[2:2 + 2 * twos:2].set(receiver + shifted)
    return sizes[jax.random.permutation(jax.random.fold_in(stream_key, 2), amount)]


def normal_values(stream_key, dims, deviation, limit, cuts=(), held_as=jnp.bfloat16):
    array = jax.random.normal(stream_key, dims, jnp.float32) * deviation
    if len(cuts) > 0:
        array = level_of(stream_key, dims, cuts, -0.22, 0.18) * array
    return jnp.clip(array, min=-limit, max=limit).astype(held_as)


def setup_inputs(seed: int = 0) -> dict:
    splits = jax.random.split(jax.random.key(seed), 10)
    return {
        "forward_rows": draw_forward_rows(jax.random.fold_in(splits[9], 71), 0),
        "saved_rows": draw_saved_rows(jax.random.fold_in(splits[9], 71), 0),
        "output_grad": normal_values(splits[2], (N_SECTION, SEQLEN, MODEL_WIDTH), 1.0, 6.0, ((0, 16), (1, 8))),
        "forward_docs": jax.vmap(lambda own: jnp.searchsorted(jnp.cumsum(ragged_sizes(own, 4, SEQLEN, SEQLEN // 2, 0)), jnp.arange(SEQLEN), side="right"))(jax.random.split(splits[3], N_SECTION)).reshape((N_SECTION, SEQLEN)).astype(jnp.int32),
        "backward_docs": jax.vmap(lambda own: jnp.searchsorted(jnp.cumsum(ragged_sizes(own, 4, SEQLEN, SEQLEN // 2, 0)), jnp.arange(SEQLEN), side="right"))(jax.random.split(splits[4], N_SECTION)).reshape((N_SECTION, SEQLEN)).astype(jnp.int32),
        "norm_gain": draw_norm_gain(jax.random.fold_in(splits[9], 71), 0),
        "query_weight": normal_values(splits[6], (N_SECTION, MODEL_WIDTH, HQ * HEAD_SIZE), MODEL_WIDTH ** -0.5, 0.09375, ((0, 16), (2, 8))),
        "key_matrix": normal_values(splits[7], (N_SECTION, MODEL_WIDTH, KEY_VALUE_HEADS * HEAD_SIZE), MODEL_WIDTH ** -0.5, 0.09375, ((0, 16), (2, 8))),
        "value_matrix": normal_values(splits[8], (N_SECTION, MODEL_WIDTH, KEY_VALUE_HEADS * HEAD_SIZE), MODEL_WIDTH ** -0.5, 0.09375, ((0, 16), (2, 8))),
    }


epsilon = 1e-05
rope_base = 500000.0

def rounded(values):
    return lax.optimization_barrier(values.astype(jnp.bfloat16))

def rotation_tables(positions):
    half = HEAD_SIZE // 2
    freqs = rope_base ** (-(jnp.arange(half, dtype=jnp.float32) * 2.0 / HEAD_SIZE))
    angles = positions[:, None] * freqs[None, :]
    return (jnp.cos(angles), jnp.sin(angles))

def rotate(values, cosines, sines, sign):
    half = values.shape[-1] // 2
    extra = (1,) * (values.ndim - 2)
    cos_wide = cosines.reshape(cosines.shape[:1] + extra + cosines.shape[1:])
    sin_wide = sines.reshape(sines.shape[:1] + extra + sines.shape[1:])
    first = values[..., :half]
    second = values[..., half:]
    return jnp.concatenate([first * cos_wide - sign * second * sin_wide, second * cos_wide + sign * first * sin_wide], axis=-1)

def project(hidden, gain_row, query_weight, key_matrix, value_matrix):
    sequence_length = hidden.shape[0]
    scale_rows = lax.rsqrt(lax.optimization_barrier(jnp.mean(hidden * hidden, axis=-1, keepdims=True)) + epsilon)
    normalized_input = rounded(hidden * scale_rows * gain_row)
    cosines, sines = rotation_tables(jnp.arange(sequence_length, dtype=jnp.float32))
    query_proj = jnp.dot(normalized_input, query_weight, preferred_element_type=jnp.float32).reshape(sequence_length, HQ, HEAD_SIZE)
    key_projected_rows = jnp.dot(normalized_input, key_matrix, preferred_element_type=jnp.float32).reshape(sequence_length, KEY_VALUE_HEADS, HEAD_SIZE)
    value_projected_rows = jnp.dot(normalized_input, value_matrix, preferred_element_type=jnp.float32).reshape(sequence_length, KEY_VALUE_HEADS, HEAD_SIZE)
    query_rows_local = rounded(rotate(query_proj, cosines, sines, 1.0))
    key_rows = rounded(rotate(key_projected_rows, cosines, sines, 1.0))
    value_rows = rounded(value_projected_rows)
    return (scale_rows, query_rows_local, key_rows, value_rows, cosines, sines)

def allowed_pairs(documents):
    sequence_length = documents.shape[0]
    positions = jnp.arange(sequence_length)
    return (positions[None, :] <= positions[:, None]) & (documents[:, None] == documents[None, :])

def group_probs(query_group, key_head, allowed):
    scores = jnp.einsum('tgd,sd->gts', query_group.astype(jnp.float32), key_head.astype(jnp.float32)) * HEAD_SIZE ** (-0.5)
    scores = jnp.where(allowed, scores, -1e+30)
    row_top = lax.optimization_barrier(jnp.max(scores, axis=-1, keepdims=True))
    exp_scores = jnp.where(allowed, jnp.exp(scores - row_top), 0.0)
    return exp_scores / lax.optimization_barrier(jnp.sum(exp_scores, axis=-1, keepdims=True))

def forward_layer(layer_rows, documents, gain_row, query_weight, key_matrix, value_matrix):
    hidden = layer_rows.astype(jnp.float32)
    sequence_length = hidden.shape[0]
    scale_rows, query_rows_local, key_rows, value_rows, cosines, sines = project(hidden, gain_row, query_weight, key_matrix, value_matrix)
    allowed = allowed_pairs(documents)
    query_head_count = query_rows_local.reshape(sequence_length, KEY_VALUE_HEADS, QUERIES_PER_KEY, HEAD_SIZE).transpose(1, 0, 2, 3)
    key_heads = key_rows.transpose(1, 0, 2)
    value_heads = value_rows.transpose(1, 0, 2)

    def one_group(operands):
        query_group, key_head, value_head = operands
        probability = rounded(group_probs(query_group, key_head, allowed))
        return rounded(jnp.einsum('gts,sd->tgd', probability.astype(jnp.float32), value_head.astype(jnp.float32)))
    outputs = lax.map(one_group, (query_head_count, key_heads, value_heads))
    outputs = outputs.transpose(1, 0, 2, 3).reshape(sequence_length, HQ * HEAD_SIZE)
    return (hidden + outputs.astype(jnp.float32)).astype(jnp.bfloat16)

def backward_layer(layer_rows, output_gradient, documents, gain_row, query_weight, key_matrix, value_matrix):
    hidden = layer_rows.astype(jnp.float32)
    sequence_length = hidden.shape[0]
    scale_rows, query_rows_local, key_rows, value_rows, cosines, sines = project(hidden, gain_row, query_weight, key_matrix, value_matrix)
    allowed = allowed_pairs(documents)
    query_head_count = query_rows_local.reshape(sequence_length, KEY_VALUE_HEADS, QUERIES_PER_KEY, HEAD_SIZE).transpose(1, 0, 2, 3)
    key_heads = key_rows.transpose(1, 0, 2)
    value_heads = value_rows.transpose(1, 0, 2)
    head_gradients = output_gradient.reshape(sequence_length, KEY_VALUE_HEADS, QUERIES_PER_KEY, HEAD_SIZE).transpose(1, 0, 2, 3)
    scale = HEAD_SIZE ** (-0.5)

    def one_group(operands):
        query_group, key_head, value_head, grad_group = operands
        probability = group_probs(query_group, key_head, allowed)
        probability_low = rounded(probability).astype(jnp.float32)
        grad_float = grad_group.astype(jnp.float32)
        grad_probs = jnp.einsum('tgd,sd->gts', grad_float, value_head.astype(jnp.float32))
        row_delta = lax.optimization_barrier(jnp.sum(probability * grad_probs, axis=-1, keepdims=True))
        grad_scores = rounded(probability * (grad_probs - row_delta)).astype(jnp.float32)
        query_grad = jnp.einsum('gts,sd->tgd', grad_scores, key_head.astype(jnp.float32)) * scale
        key_grad = jnp.einsum('gts,tgd->sd', grad_scores, query_group.astype(jnp.float32)) * scale
        value_grad = jnp.einsum('gts,tgd->sd', probability_low, grad_float)
        return (rounded(rotate(query_grad, cosines, sines, -1.0)), rounded(rotate(key_grad, cosines, sines, -1.0)), rounded(value_grad))
    query_grads, key_gradient_rows, value_gradient_rows = lax.map(one_group, (query_head_count, key_heads, value_heads, head_gradients))
    query_grads = query_grads.transpose(1, 0, 2, 3).reshape(sequence_length, HQ * HEAD_SIZE)
    key_gradient_rows = key_gradient_rows.transpose(1, 0, 2).reshape(sequence_length, KEY_VALUE_HEADS * HEAD_SIZE)
    value_gradient_rows = value_gradient_rows.transpose(1, 0, 2).reshape(sequence_length, KEY_VALUE_HEADS * HEAD_SIZE)
    query_cols = HQ * HEAD_SIZE // N_SEQ
    pair_columns = KEY_VALUE_HEADS * HEAD_SIZE // N_SEQ
    input_sum = jnp.zeros((sequence_length, MODEL_WIDTH), jnp.float32)
    for index in range(N_SEQ):
        query_slice = slice(index * query_cols, (index + 1) * query_cols)
        pair_slice = slice(index * pair_columns, (index + 1) * pair_columns)
        term = jnp.dot(query_grads[:, query_slice], query_weight[:, query_slice].T, preferred_element_type=jnp.float32)
        term = term + jnp.dot(key_gradient_rows[:, pair_slice], key_matrix[:, pair_slice].T, preferred_element_type=jnp.float32)
        term = term + jnp.dot(value_gradient_rows[:, pair_slice], value_matrix[:, pair_slice].T, preferred_element_type=jnp.float32)
        input_sum = input_sum + rounded(term).astype(jnp.float32)
    gained = gain_row * input_sum
    inner_sum = lax.optimization_barrier(jnp.sum(hidden * gained, axis=-1, keepdims=True))
    norm_part = scale_rows * gained - hidden * (scale_rows * scale_rows * scale_rows) * inner_sum / MODEL_WIDTH
    return (output_gradient.astype(jnp.float32) + norm_part).astype(jnp.bfloat16)

def run_forward(operands):
    layer_rows, documents, gain_row, query_weight, key_matrix, value_matrix = operands
    return forward_layer(layer_rows, documents, gain_row, query_weight, key_matrix, value_matrix)

def run_backward(operands):
    layer_rows, output_gradient, documents, gain_row, query_weight, key_matrix, value_matrix = operands
    return backward_layer(layer_rows, output_gradient, documents, gain_row, query_weight, key_matrix, value_matrix)

def reference(forward_rows, saved_rows, output_grad, forward_docs, backward_docs, norm_gain, query_weight, key_matrix, value_matrix):
    first_out = lax.map(run_forward, (forward_rows, forward_docs, norm_gain, query_weight, key_matrix, value_matrix))
    first_grad = lax.map(run_backward, (saved_rows, output_grad, backward_docs, norm_gain, query_weight, key_matrix, value_matrix))
    empty_rows = jnp.zeros_like(first_out[:1])
    section_output = jnp.concatenate([empty_rows, first_out[:-1]], axis=0)
    input_grad = jnp.concatenate([first_grad[1:], empty_rows], axis=0)
    return (section_output, input_grad)
```

```python
import jax
import jax.numpy as jnp
from jax import lax
from jax.sharding import PartitionSpec as P

MODEL_WIDTH = 4096
HEAD_SIZE = 128


epsilon = 1e-05
rope_base = 500000.0


def passed_along(shard, axis, by):
    peers = lax.axis_size(axis)
    pairs = [(i, i + by) for i in range(peers) if 0 <= i + by < peers]
    return lax.ppermute(shard, axis, pairs)


def rotation_tables(positions):
    half = HEAD_SIZE // 2
    freqs = rope_base ** (-(jnp.arange(half, dtype=jnp.float32) * 2.0 / HEAD_SIZE))
    angles = positions[:, None] * freqs[None, :]
    return (jnp.cos(angles), jnp.sin(angles))


def rotate(values, cosines, sines, sign):
    half = values.shape[-1] // 2
    extra = (1,) * (values.ndim - 2)
    cos_wide = cosines.reshape(cosines.shape[:1] + extra + cosines.shape[1:])
    sin_wide = sines.reshape(sines.shape[:1] + extra + sines.shape[1:])
    first = values[..., :half]
    second = values[..., half:]
    return jnp.concatenate(
        [first * cos_wide - sign * second * sin_wide, second * cos_wide + sign * first * sin_wide],
        axis=-1,
    )


def pair_mask(row_docs, col_docs, row_begin):
    row_pos = row_begin + lax.iota(jnp.int32, row_docs.shape[0])
    col_pos = lax.iota(jnp.int32, col_docs.shape[0])
    return (col_pos[None, :] <= row_pos[:, None]) & (row_docs[:, None] == col_docs[None, :])


def block_probs(query_block, key_heads, allowed):
    scores = jnp.einsum(
        "tjgd,sjd->jgts", query_block, key_heads, preferred_element_type=jnp.float32
    ) * HEAD_SIZE ** (-0.5)
    scores = jnp.where(allowed, scores, -1e30)
    row_top = jnp.max(scores, axis=-1, keepdims=True)
    exp_scores = jnp.where(allowed, jnp.exp(scores - row_top), 0.0)
    return exp_scores / jnp.sum(exp_scores, axis=-1, keepdims=True)


def attend(query_rows_local, key_rows, value_rows, documents):
    sequence_length = query_rows_local.shape[0]
    groups = key_rows.shape[1] // HEAD_SIZE
    group_size = query_rows_local.shape[1] // key_rows.shape[1]
    query_head_count = query_rows_local.reshape(sequence_length, groups, group_size, HEAD_SIZE)
    key_heads = key_rows.reshape(sequence_length, groups, HEAD_SIZE)
    value_heads = value_rows.reshape(sequence_length, groups, HEAD_SIZE)
    block_rows = min(512, sequence_length)
    pieces = []
    for block_index in range(sequence_length // block_rows):
        begin_row = block_index * block_rows
        end_row = begin_row + block_rows
        allowed = pair_mask(documents[begin_row:end_row], documents[:end_row], begin_row)
        probability = block_probs(
            query_head_count[begin_row:end_row], key_heads[:end_row], allowed
        ).astype(jnp.bfloat16)
        mixed_rows = jnp.einsum(
            "jgts,sjd->tjgd", probability, value_heads[:end_row], preferred_element_type=jnp.float32
        )
        pieces.append(mixed_rows.astype(jnp.bfloat16))
    return lax.optimization_barrier(
        jnp.concatenate(pieces, 0).reshape(sequence_length, query_rows_local.shape[1])
    )


def attend_back(query_rows_local, key_rows, value_rows, output_gradient, documents, cosines, sines):
    sequence_length = query_rows_local.shape[0]
    groups = key_rows.shape[1] // HEAD_SIZE
    group_size = query_rows_local.shape[1] // key_rows.shape[1]
    query_head_count = query_rows_local.reshape(sequence_length, groups, group_size, HEAD_SIZE)
    key_heads = key_rows.reshape(sequence_length, groups, HEAD_SIZE)
    value_heads = value_rows.reshape(sequence_length, groups, HEAD_SIZE)
    head_gradients = output_gradient.reshape(sequence_length, groups, group_size, HEAD_SIZE)
    scale = HEAD_SIZE ** (-0.5)
    key_grad = jnp.zeros((sequence_length, groups, HEAD_SIZE), jnp.float32)
    value_grad = jnp.zeros((sequence_length, groups, HEAD_SIZE), jnp.float32)
    block_rows = min(512, sequence_length)
    query_pieces = []
    for block_index in range(sequence_length // block_rows):
        begin_row = block_index * block_rows
        end_row = begin_row + block_rows
        allowed = pair_mask(documents[begin_row:end_row], documents[:end_row], begin_row)
        query_block = query_head_count[begin_row:end_row]
        grad_block = head_gradients[begin_row:end_row]
        probability = block_probs(query_block, key_heads[:end_row], allowed)
        grad_probs = jnp.einsum(
            "tjgd,sjd->jgts", grad_block, value_heads[:end_row], preferred_element_type=jnp.float32
        )
        row_delta = jnp.sum(probability * grad_probs, axis=-1, keepdims=True)
        grad_scores = (probability * (grad_probs - row_delta)).astype(jnp.bfloat16)
        query_piece = (
            jnp.einsum(
                "jgts,sjd->tjgd",
                grad_scores,
                key_heads[:end_row],
                preferred_element_type=jnp.float32,
            )
            * scale
        )
        query_piece = rotate(
            query_piece, cosines[begin_row:end_row], sines[begin_row:end_row], -1.0
        )
        query_pieces.append(query_piece.astype(jnp.bfloat16))
        key_grad = key_grad.at[:end_row].add(
            jnp.einsum(
                "jgts,tjgd->sjd", grad_scores, query_block, preferred_element_type=jnp.float32
            )
            * scale
        )
        value_grad = value_grad.at[:end_row].add(
            jnp.einsum(
                "jgts,tjgd->sjd",
                probability.astype(jnp.bfloat16),
                grad_block,
                preferred_element_type=jnp.float32,
            )
        )
    query_grad = jnp.concatenate(query_pieces, 0).reshape(
        sequence_length, query_rows_local.shape[1]
    )
    key_grad = (
        rotate(key_grad, cosines, sines, -1.0)
        .astype(jnp.bfloat16)
        .reshape(sequence_length, groups * HEAD_SIZE)
    )
    value_grad = value_grad.astype(jnp.bfloat16).reshape(sequence_length, groups * HEAD_SIZE)
    return lax.optimization_barrier((query_grad, key_grad, value_grad))


def token_scale(hidden):
    return lax.rsqrt(jnp.mean(hidden * hidden, axis=-1, keepdims=True) + epsilon)


def hop_x(shard, by):
    pairs = [(i, (i + 2 * by) % 8) for i in range(8)]
    return lax.ppermute(shard, "seq", pairs)


def hop_z(shard):
    return lax.ppermute(shard, "seq", [(i, i ^ 1) for i in range(8)])


def ring_gather(blocks):
    near = []
    for block in blocks:
        near.append((hop_x(block, 1), hop_x(block, -1)))
    far = []
    for from_left, from_right in near:
        half = from_left.shape[0] // 2
        far.append((hop_x(from_left[:half], 1), hop_x(from_right[half:], -1)))
    rows = list(blocks)
    rows += [pair[1] for pair in near]
    for pair in far:
        rows += list(pair)
    rows += [pair[0] for pair in near]
    return rows


def gather_rows(block):
    return jnp.concatenate(ring_gather([block, hop_z(block)]), 0)


def local_positions(x, z, rows):
    offset = jnp.arange(8)
    owner = ((x + offset // 2) % 4) * 2 + (z ^ (offset % 2))
    return (owner[:, None] * rows + jnp.arange(rows)[None, :]).reshape(-1)


def in_order(local, x, z):
    width = local.shape[1]
    split = local.reshape(4, 2, -1, width)
    split = jnp.where(z == 1, split[:, ::-1], split)
    twice = jnp.concatenate([split, split], 0)
    start = (4 - x) % 4
    return lax.dynamic_slice_in_dim(twice, start, 4, 0).reshape(-1, width)


def heads_inputs(rows_local, weight, x, z):
    positions = local_positions(x, z, rows_local.shape[0] // 8)
    cosines, sines = rotation_tables(positions.astype(jnp.float32))
    count = rows_local.shape[0]
    projected = jnp.dot(rows_local, weight, preferred_element_type=jnp.float32)
    turned = rotate(projected[:, :640].reshape(count, -1, HEAD_SIZE), cosines, sines, 1.0)
    together = jnp.concatenate(
        [turned.reshape(count, -1).astype(jnp.bfloat16), projected[:, 640:].astype(jnp.bfloat16)], 1
    )
    together = in_order(lax.optimization_barrier(together), x, z)
    return (together[:, :512], together[:, 512:640], together[:, 640:])


def reduce_rows(grads, weight, x, z):
    unit = grads.shape[0] // 4

    def share(offset):
        rows = lax.dynamic_slice_in_dim(grads, ((x + offset) % 4) * unit, unit, 0)
        return jnp.einsum(
            "tc,rc->tr", rows, weight, preferred_element_type=jnp.float32
        ).astype(jnp.bfloat16)

    half = unit // 2
    opposite = share(2)
    passed_right = hop_x(opposite[:half], 1)
    passed_left = hop_x(opposite[half:], -1)
    right = share(1)
    left = share(3)

    def joined(a, b):
        return (a.astype(jnp.float32) + b.astype(jnp.float32)).astype(jnp.bfloat16)

    got_left_plain = hop_x(right[half:], 1)
    got_right_plain = hop_x(left[:half], -1)
    got_left_sum = hop_x(joined(right[:half], passed_right), 1)
    got_right_sum = hop_x(joined(left[half:], passed_left), -1)
    own = share(0).astype(jnp.float32)
    top = own[:half] + got_left_sum.astype(jnp.float32) + got_right_plain.astype(jnp.float32)
    bottom = own[half:] + got_left_plain.astype(jnp.float32) + got_right_sum.astype(jnp.float32)
    mine = jnp.where(z == 0, top, bottom)
    other = jnp.where(z == 0, bottom, top).astype(jnp.bfloat16)
    return mine + hop_z(other).astype(jnp.float32)


def body(
    forward_rows,
    saved_rows,
    output_grad,
    forward_docs,
    backward_docs,
    norm_gain,
    query_weight,
    key_matrix,
    value_matrix,
):
    section_index = lax.axis_index("section")
    seq_index = lax.axis_index("seq")
    x, z = seq_index // 2, seq_index % 2
    first_docs = lax.dynamic_index_in_dim(forward_docs, section_index, 0, keepdims=False)
    back_docs = lax.dynamic_index_in_dim(backward_docs, section_index, 0, keepdims=False)
    gain_row = norm_gain[0]
    weight = jnp.concatenate([query_weight[0], key_matrix[0], value_matrix[0]], 1)
    forward_hidden = forward_rows[0].astype(jnp.float32)
    forward_normed = (forward_hidden * token_scale(forward_hidden) * gain_row).astype(jnp.bfloat16)
    back_hidden = saved_rows[0].astype(jnp.float32)
    back_scale = token_scale(back_hidden)
    back_normed = (back_hidden * back_scale * gain_row).astype(jnp.bfloat16)
    forward_local = gather_rows(forward_normed)
    forward_local, back_normed = lax.optimization_barrier((forward_local, back_normed))
    back_local = gather_rows(back_normed)
    query_rows_local, key_rows, value_rows = heads_inputs(forward_local, weight, x, z)
    mixed_rows = attend(query_rows_local, key_rows, value_rows, first_docs)
    mixed_rows = lax.all_to_all(mixed_rows, "seq", split_axis=0, concat_axis=1, tiled=True)
    first_out = (forward_hidden + mixed_rows.astype(jnp.float32)).astype(jnp.bfloat16)
    section_output = passed_along(first_out, "section", 1)
    head_gradients = lax.all_to_all(output_grad[0], "seq", split_axis=1, concat_axis=0, tiled=True)
    query_rows_local, key_rows, value_rows = heads_inputs(back_local, weight, x, z)
    cosines, sines = rotation_tables(jnp.arange(query_rows_local.shape[0], dtype=jnp.float32))
    query_grad, key_grad, value_grad = attend_back(
        query_rows_local, key_rows, value_rows, head_gradients, back_docs, cosines, sines
    )
    grads = jnp.concatenate([query_grad, key_grad, value_grad], 1)
    input_sum = reduce_rows(grads, weight, x, z)
    gained = gain_row * input_sum
    inner_sum = jnp.sum(back_hidden * gained, axis=-1, keepdims=True)
    norm_part = (
        back_scale * gained
        - back_hidden * (back_scale * back_scale * back_scale) * inner_sum / MODEL_WIDTH
    )
    first_grad = (output_grad[0].astype(jnp.float32) + norm_part).astype(jnp.bfloat16)
    input_grad = passed_along(first_grad, "section", -1)
    return (section_output[None], input_grad[None])


def solution(mesh):
    placed = (
        P("section", "seq", None),
        P("section", "seq", None),
        P("section", "seq", None),
        P(),
        P(),
        P("section", None),
        P("section", None, "seq"),
        P("section", None, "seq"),
        P("section", None, "seq"),
    )
    return jax.shard_map(
        body,
        mesh=mesh,
        in_specs=placed,
        out_specs=(P("section", "seq", None), P("section", "seq", None)),
        check_vma=False,
    )
```
